32 devices in a mesh: head: 8 (over z, x), ctx: 4 (over y, core).
Axes of the slice: x: 2, y: 2, z: 4, core: 2. Of those that a mesh axis runs over, the one named last changes fastest.
Arguments:
- queries: bfloat16 [768, 16384], P('ctx', 'head'), may hold values from -12 to 12
- rotated_key_rows: bfloat16 [768, 1024], P('ctx'), may hold values from -5 to 5
- value_state_rows: bfloat16 [768, 1024], P('ctx'), may hold values from -6 to 6
- positions: int32 [768], P('ctx'), may hold values from 0 to 767, as said below
Outputs:
- attended: bfloat16 [768, 16384], P('ctx', 'head')
The draws below stay inside these ranges and needn't reach their ends.
Inputs may be any that keep to these rules, and one draw needn't show every extreme that they name: Each aligned block of 96 rows holds 96 consecutive positions in ascending order; the blocks' starts are a permutation of the multiples of 96.
All inputs are finite; a program needn't handle non-finite values.
Results may differ from the reference program's by a relative error of at most 0.0054.
Values may be sent and summed in bfloat16 or wider, within the bound.
No kernel may reach another device: no remote copies, remote signals or barrier semaphores. Data moves between devices by JAX's collectives and lax.ppermute only.
A program may use at most 64 MiB of HBM per device.

```python
import jax
import jax.numpy as jnp
from jax import lax

HEAD_SIZE = 128
QUERY_HEAD_COUNT = 128
KEY_VALUE_HEADS = 8
SPAN = 96
QUERIES_PER_KV = 16
SPANS = 8
TOKEN_COUNT = 768


def draw_queries(key, part):
    base_offset = jnp.clip(2.5 * jax.random.normal(jax.random.fold_in(key, 11), (TOKEN_COUNT, QUERY_HEAD_COUNT * HEAD_SIZE), jnp.float32), -12.0, 12.0)
    return base_offset.astype(jnp.bfloat16)


def draw_rotated_key_rows(key, part):
    base_offset = jnp.clip(jax.random.normal(jax.random.fold_in(key, 13), (TOKEN_COUNT, KEY_VALUE_HEADS * HEAD_SIZE), jnp.float32), -5.0, 5.0)
    return base_offset.astype(jnp.bfloat16)


def draw_positions(key, part):
    order = jax.random.permutation(jax.random.fold_in(key, 3), SPANS)
    indices = jnp.arange(TOKEN_COUNT, dtype=jnp.int32)
    return (order[indices // SPAN] * SPAN + indices % SPAN).astype(jnp.int32)


def level_of(key, extent, cuts, least, largest):
    loudness = 1.0
    for dim, shards_of in cuts:
        steps = jax.random.uniform(jax.random.fold_in(jax.random.fold_in(key, 6), dim), (shards_of,), jnp.float32, least / len(cuts), largest / len(cuts))
        loudness = loudness * jnp.repeat(jnp.exp(steps), extent[dim] // shards_of).reshape((-1,) + (1,) * (len(extent) - 1 - dim))
    return loudness


def scatter_about(key, shape, deviation, bound, shards=(), kind=jnp.bfloat16):
    loudness = level_of(key, shape, shards, -0.22, 0.18) if shards else 1.0
    array = jax.random.normal(key, shape, jnp.float32) * deviation * loudness
    return jnp.minimum(jnp.maximum(array, -bound), bound).astype(kind)


def setup_inputs(seed: int = 0) -> dict:
    streams_of = jax.random.split(jax.random.key(seed), 5)
    return {
        "queries": draw_queries(jax.random.fold_in(streams_of[4], 71), 0),
        "rotated_key_rows": draw_rotated_key_rows(jax.random.fold_in(streams_of[4], 71), 0),
        "value_state_rows": scatter_about(streams_of[2], (TOKEN_COUNT, KEY_VALUE_HEADS * HEAD_SIZE), 1.0, 6.0, ((0, 4),)),
        "positions": draw_positions(jax.random.fold_in(streams_of[4], 71), 0),
    }


negative_fill = -1e30


def reference(queries, rotated_key_rows, value_state_rows, positions):
    scale_value = HEAD_SIZE ** -0.5
    query_heads = queries.reshape(TOKEN_COUNT, QUERY_HEAD_COUNT, HEAD_SIZE).transpose(1, 0, 2)
    key_head_rows = rotated_key_rows.reshape(TOKEN_COUNT, KEY_VALUE_HEADS, HEAD_SIZE).transpose(1, 0, 2)
    value_head_rows = value_state_rows.reshape(TOKEN_COUNT, KEY_VALUE_HEADS, HEAD_SIZE).transpose(1, 0, 2)
    allowed = positions[None, :] <= positions[:, None]

    def one_head(pair):
        head_query, head_number = pair
        group_index = head_number // QUERIES_PER_KV
        scores = jnp.dot(head_query, key_head_rows[group_index].T, preferred_element_type=jnp.float32) * scale_value
        scores = jnp.where(allowed, scores, negative_fill)
        highest = scores.max(-1, keepdims=True)
        weights = jnp.where(allowed, jnp.exp(scores - highest), 0.0)
        total = weights.sum(-1, keepdims=True)
        mixed = jnp.dot(weights.astype(jnp.bfloat16), value_head_rows[group_index], preferred_element_type=jnp.float32)
        return (mixed / total).astype(jnp.bfloat16)

    outputs = lax.map(one_head, (query_heads, jnp.arange(QUERY_HEAD_COUNT, dtype=jnp.int32)))
    return outputs.transpose(1, 0, 2).reshape(TOKEN_COUNT, QUERY_HEAD_COUNT * HEAD_SIZE)
```

```python
import functools

import jax
import jax.numpy as jnp
from jax import lax
from jax.experimental import pallas as pl
from jax.experimental.pallas import tpu as pltpu
from jax.sharding import PartitionSpec as P

HEAD_SIZE = 128
QUERIES_PER_KV = 16
SPAN = 96
SCALE = HEAD_SIZE ** (-0.5)
SCALE_TWO = SCALE * 1.4426950408889634
ONES_ROWS = 16
negative_fill = -1e30
LEAST_TOTAL = 1e-25
LARGEST_TOTAL = 1e25

f32 = jnp.float32
bf16 = jnp.bfloat16


def nt(a, b):
    return lax.dot_general(a, b, (((1,), (1,)), ((), ())), preferred_element_type=f32)


def attention(group_blocks, positions_ref, q_ref, *refs):
    *payloads, out_ref, keys_ref, values_ref, spans_ref, acc_ref = refs
    rows = q_ref.shape[0]
    heads = q_ref.shape[1] // HEAD_SIZE
    spans = rows // SPAN
    block = rows + ONES_ROWS
    blocks = [(ref, i) for ref in payloads for i in range(ref.shape[0] // block)]
    keys = len(blocks) * rows
    width = heads * SPAN
    group = group_blocks * rows
    groups = keys // group

    for at, (ref, i) in enumerate(blocks):
        top, here = i * block, slice(at * rows, (at + 1) * rows)
        keys_ref[here, :] = ref[top : top + rows, :HEAD_SIZE]
        values_ref[:HEAD_SIZE, here] = ref[top : top + rows, HEAD_SIZE:].T
        spans_ref[:, here] = jnp.broadcast_to(ref[top + rows : top + rows + 1, :rows], (ONES_ROWS, rows))
    values_ref[HEAD_SIZE:, :] = jnp.ones((ONES_ROWS, keys), bf16)

    def triangle(columns):
        key = lax.broadcasted_iota(jnp.int32, (SPAN, columns), 0)
        query = lax.broadcasted_iota(jnp.int32, (SPAN, columns), 1) % SPAN
        return key <= query

    fine = None
    for s in range(spans):
        here = slice(s * SPAN, (s + 1) * SPAN)
        span = (positions_ref[s * SPAN] // SPAN).astype(f32)
        q = jnp.concatenate(
            [q_ref[here, h * HEAD_SIZE : (h + 1) * HEAD_SIZE] for h in range(heads)], 0
        )

        def part(first, own):
            allowed = (spans_ref[:, pl.ds(first, group)].astype(f32) <= span).astype(f32).astype(bf16)
            values = values_ref[:, pl.ds(first, group)] * allowed[:1]
            weights = jnp.exp2(nt(keys_ref[pl.ds(first, group), :], q) * SCALE_TWO)
            if own:
                diagonal = jnp.where(triangle(width), weights[here], 0.0)
                pieces = [weights[: s * SPAN], diagonal, weights[(s + 1) * SPAN :]]
                weights = jnp.concatenate([p for p in pieces if p.shape[0]], 0)
            return jnp.dot(values, weights.astype(bf16), preferred_element_type=f32)

        summed = part(0, True)
        if groups > 1:
            acc_ref[...] = summed

            @pl.loop(1, groups)
            def _(g):
                acc_ref[...] += part(pl.multiple_of(g * group, group), False)

            summed = acc_ref[...]
        total = summed[HEAD_SIZE : HEAD_SIZE + 1]
        inside = jnp.where((total >= LEAST_TOTAL) & (total <= LARGEST_TOTAL), 1.0, 0.0)
        fine = inside if fine is None else jnp.minimum(fine, inside)
        attended = (summed[:HEAD_SIZE] / total).T.astype(bf16)
        for h in range(heads):
            out_ref[here, h * HEAD_SIZE : (h + 1) * HEAD_SIZE] = attended[h * SPAN : (h + 1) * SPAN]

    @pl.when(jnp.min(fine) < 0.5)
    def _():
        def head(h, carry):
            at = pl.ds(pl.multiple_of(h * HEAD_SIZE, HEAD_SIZE), HEAD_SIZE)
            for s in range(spans):
                here = slice(s * SPAN, (s + 1) * SPAN)
                span = (positions_ref[s * SPAN] // SPAN).astype(f32)
                q = q_ref[here, at]

                def part(g, state):
                    highest, summed = state
                    first = pl.multiple_of(g * group, group)
                    place = spans_ref[:1, pl.ds(first, group)].astype(f32)
                    column = jnp.broadcast_to(place, (HEAD_SIZE, group)).T[:, :SPAN]
                    key = lax.broadcasted_iota(jnp.int32, (group, SPAN), 0) + first
                    query = lax.broadcasted_iota(jnp.int32, (group, SPAN), 1) + s * SPAN
                    later = (key >= s * SPAN) & (key < (s + 1) * SPAN) & (key > query)
                    allowed = (column <= span) & jnp.logical_not(later)
                    scores = nt(keys_ref[pl.ds(first, group), :], q) * SCALE
                    scores = jnp.where(allowed, scores, negative_fill)
                    newest = jnp.maximum(highest, jnp.max(scores, 0, keepdims=True))
                    weights = jnp.where(allowed, jnp.exp(scores - newest), 0.0).astype(bf16)
                    summed = summed * jnp.exp(highest - newest) + jnp.dot(
                        values_ref[:, pl.ds(first, group)], weights, preferred_element_type=f32
                    )
                    return newest, summed

                state = (
                    jnp.full((1, SPAN), negative_fill, f32),
                    jnp.zeros((HEAD_SIZE + ONES_ROWS, SPAN), f32),
                )
                summed = lax.fori_loop(0, groups, part, state)[1]
                out_ref[here, at] = (summed[:HEAD_SIZE] / summed[HEAD_SIZE : HEAD_SIZE + 1]).T.astype(bf16)
            return carry

        lax.fori_loop(0, heads, head, 0)


def attend(queries, positions, payloads, group_blocks):
    rows = queries.shape[0]
    heads = queries.shape[1] // HEAD_SIZE
    keys = sum(p.shape[0] for p in payloads) // (rows + ONES_ROWS) * rows
    vmem = pl.BlockSpec(memory_space=pltpu.VMEM)
    return pl.pallas_call(
        functools.partial(attention, group_blocks),
        out_shape=jax.ShapeDtypeStruct(queries.shape, bf16),
        in_specs=[pl.BlockSpec(memory_space=pltpu.SMEM)] + [vmem] * (1 + len(payloads)),
        out_specs=vmem,
        scratch_shapes=[
            pltpu.VMEM((keys, HEAD_SIZE), bf16),
            pltpu.VMEM((HEAD_SIZE + ONES_ROWS, keys), bf16),
            pltpu.VMEM((ONES_ROWS, keys), bf16),
            pltpu.VMEM((HEAD_SIZE + ONES_ROWS, heads * SPAN), f32),
        ],
        compiler_params=pltpu.CompilerParams(vmem_limit_bytes=40 << 20),
    )(positions, queries, *payloads)


def swapped(block, bit):
    devices = range(lax.axis_size("ctx"))
    return lax.ppermute(block, "ctx", [(i ^ bit, i) for i in devices])


def body(queries, rotated_key_rows, value_state_rows, positions):
    row_count = queries.shape[0]
    heads_here = queries.shape[1] // HEAD_SIZE
    group_index = lax.axis_index("head") * heads_here // QUERIES_PER_KV
    key_slice = lax.dynamic_slice_in_dim(rotated_key_rows, group_index * HEAD_SIZE, HEAD_SIZE, 1)
    value_slice = lax.dynamic_slice_in_dim(value_state_rows, group_index * HEAD_SIZE, HEAD_SIZE, 1)
    own_rows = jnp.concatenate([key_slice, value_slice], 1)
    spans = jnp.pad((positions // SPAN).astype(bf16)[None], ((0, ONES_ROWS - 1), (0, 2 * HEAD_SIZE - row_count)))
    own = jnp.concatenate([own_rows, spans], 0)
    if lax.axis_size("ctx") == 4:
        core = swapped(own, 1)
        chip = swapped(own, 2)
        both = swapped(chip, 1)
        payloads = [own, core, chip, both]
    else:
        size = lax.axis_size("ctx")
        everyone = lax.all_gather(own, "ctx", axis=0)
        others = (lax.axis_index("ctx") + jnp.arange(size)) % size
        payloads = [jnp.take(everyone, others, axis=0).reshape(-1, 2 * HEAD_SIZE)]
    return attend(queries, positions, payloads, 4)


def solution(mesh):
    placed = (P("ctx", "head"), P("ctx", None), P("ctx", None), P("ctx"))
    return jax.shard_map(
        body, mesh=mesh, in_specs=placed, out_specs=P("ctx", "head"), check_vma=False
    )
```

```python
import functools

import jax
import jax.numpy as jnp
from jax import lax
from jax.experimental import pallas as pl
from jax.experimental.pallas import tpu as pltpu
from jax.sharding import PartitionSpec as P

HEAD_SIZE = 128
QUERIES_PER_KV = 16
SPAN = 96
SCALE = HEAD_SIZE ** (-0.5)
SCALE_TWO = SCALE * 1.4426950408889634
TAIL = 16
SUMS = HEAD_SIZE + TAIL
negative_fill = -1e30
LEAST_TOTAL = 1e-25
LARGEST_TOTAL = 1e25
VMEM_LIMIT = 40 << 20

f32 = jnp.float32
bf16 = jnp.bfloat16
in_vmem = pl.BlockSpec(memory_space=pltpu.VMEM)
in_hbm = pl.BlockSpec(memory_space=pltpu.HBM)


def nt(a, b):
    return lax.dot_general(a, b, (((1,), (1,)), ((), ())), preferred_element_type=f32)


def pack(keys, values, positions, heads):
    rows = keys.shape[0]
    group = lax.axis_index("head") * heads // QUERIES_PER_KV
    ours = [lax.dynamic_slice_in_dim(a, group * HEAD_SIZE, HEAD_SIZE, 1) for a in (keys, values)]
    *ours, positions = lax.optimization_barrier((*ours, positions))
    places = (positions // SPAN).astype(bf16)[None]
    places = jnp.pad(places, ((0, TAIL - 1), (0, 2 * HEAD_SIZE - rows)))
    return jnp.concatenate([jnp.concatenate(ours, 1), places], 0)


def blocks_of(payloads, rows):
    return [
        (ref, i * (rows + TAIL)) for ref in payloads for i in range(ref.shape[0] // (rows + TAIL))
    ]


def unpack(payloads, rows, keys_ref, values_ref, spans_ref):
    for at, (ref, top) in enumerate(blocks_of(payloads, rows)):
        here = slice(at * rows, (at + 1) * rows)
        keys_ref[here, :] = ref[top : top + rows, :HEAD_SIZE]
        values_ref[:HEAD_SIZE, here] = ref[top : top + rows, HEAD_SIZE:].T
        spans_ref[:, here] = ref[top + rows : top + rows + TAIL, :rows]
    values_ref[HEAD_SIZE:, :] = jnp.ones((TAIL, values_ref.shape[1]), bf16)


def stacked(q_ref, s, heads):
    here = slice(s * SPAN, (s + 1) * SPAN)
    return jnp.concatenate(
        [q_ref[here, h * HEAD_SIZE : (h + 1) * HEAD_SIZE] for h in range(heads)], 0
    )


def part(q, span, first, count, keys_ref, values_ref, spans_ref, own=None):
    some = pl.ds(first, count)
    allowed = (spans_ref[:1, some].astype(f32) <= span).astype(f32).astype(bf16)
    values = values_ref[:, some] * allowed
    weights = jnp.exp2(nt(keys_ref[some, :], q) * SCALE_TWO)
    if own is not None:
        key = lax.broadcasted_iota(jnp.int32, (SPAN, q.shape[0]), 0)
        query = lax.broadcasted_iota(jnp.int32, (SPAN, q.shape[0]), 1) % SPAN
        low, high = own * SPAN, (own + 1) * SPAN
        pieces = [weights[:low], jnp.where(key <= query, weights[low:high], 0.0), weights[high:]]
        weights = jnp.concatenate([p for p in pieces if p.shape[0]], 0)
    return jnp.dot(values, weights.astype(bf16), preferred_element_type=f32)


def first_kernel(queries_ref, *refs):
    *payloads, sums_ref, q_ref, keys_ref, values_ref, spans_ref, sems = refs
    rows = q_ref.shape[0]
    heads = q_ref.shape[1] // HEAD_SIZE
    copies = []
    for s in range(rows // SPAN):
        here = pl.ds(s * SPAN, SPAN)
        copies.append(pltpu.make_async_copy(queries_ref.at[here, :], q_ref.at[here, :], sems.at[s]))
        copies[-1].start()
    unpack(payloads, rows, keys_ref, values_ref, spans_ref)
    for s in range(rows // SPAN):
        copies[s].wait()
        span = spans_ref[:1, s * SPAN : s * SPAN + 1].astype(f32)
        sums_ref[s] = part(
            stacked(q_ref, s, heads), span, 0, keys_ref.shape[0], keys_ref, values_ref, spans_ref, s
        )


def first_part(queries, payloads):
    rows = queries.shape[0]
    heads = queries.shape[1] // HEAD_SIZE
    keys = sum(p.shape[0] for p in payloads) // (rows + TAIL) * rows
    return pl.pallas_call(
        first_kernel,
        out_shape=(
            jax.ShapeDtypeStruct((rows // SPAN, SUMS, heads * SPAN), f32),
            jax.ShapeDtypeStruct(queries.shape, bf16),
        ),
        in_specs=[in_hbm] + [in_vmem] * len(payloads),
        out_specs=(in_vmem, in_vmem),
        scratch_shapes=[
            pltpu.VMEM((keys, HEAD_SIZE), bf16),
            pltpu.VMEM((SUMS, keys), bf16),
            pltpu.VMEM((TAIL, keys), bf16),
            pltpu.SemaphoreType.DMA((rows // SPAN,)),
        ],
        compiler_params=pltpu.CompilerParams(vmem_limit_bytes=VMEM_LIMIT),
        cost_estimate=pl.CostEstimate(
            flops=4 * rows * heads * keys * HEAD_SIZE,
            bytes_accessed=4 * rows * heads * HEAD_SIZE,
            transcendentals=rows * heads * keys,
        ),
    )(queries, *payloads)


def last_kernel(held, group, sums_ref, q_ref, *refs):
    *payloads, out_ref, keys_ref, values_ref, spans_ref, acc_ref, ready_ref, sems = refs
    rows = q_ref.shape[0]
    heads = q_ref.shape[1] // HEAD_SIZE
    spans = rows // SPAN
    own = payloads[0]
    unpack(payloads[held:], rows, keys_ref, values_ref, spans_ref)
    groups = keys_ref.shape[0] // group

    def copy(s):
        here = pl.ds(s * SPAN, SPAN)
        return pltpu.make_async_copy(ready_ref.at[here, :], out_ref.at[here, :], sems.at[s])

    fine = None
    for s in range(spans):
        here = slice(s * SPAN, (s + 1) * SPAN)
        span = own[rows : rows + 1, s * SPAN : s * SPAN + 1].astype(f32)
        q = stacked(q_ref, s, heads)
        summed = sums_ref[s] + part(q, span, 0, group, keys_ref, values_ref, spans_ref)
        if groups > 1:
            acc_ref[...] = summed

            @pl.loop(1, groups)
            def _(g):
                first = pl.multiple_of(g * group, group)
                acc_ref[...] += part(q, span, first, group, keys_ref, values_ref, spans_ref)

            summed = acc_ref[...]
        total = summed[HEAD_SIZE : HEAD_SIZE + 1]
        inside = jnp.where((total >= LEAST_TOTAL) & (total <= LARGEST_TOTAL), 1.0, 0.0)
        fine = inside if fine is None else jnp.minimum(fine, inside)
        attended = (summed[:HEAD_SIZE] * (1.0 / total)).T.astype(bf16)
        for h in range(heads):
            ready_ref[here, h * HEAD_SIZE : (h + 1) * HEAD_SIZE] = attended[h * SPAN : (h + 1) * SPAN]
        copy(s).start()
    for s in range(spans):
        copy(s).wait()

    @pl.when(jnp.min(fine) < 0.5)
    def _():
        @pl.loop(0, heads)
        def _(h):
            at = pl.ds(pl.multiple_of(h * HEAD_SIZE, HEAD_SIZE), HEAD_SIZE)
            for s in range(spans):
                careful(payloads, q_ref, ready_ref, s, at)

        for s in range(spans):
            copy(s).start()
        for s in range(spans):
            copy(s).wait()


def careful(payloads, q_ref, ready_ref, s, at):
    rows = q_ref.shape[0]
    own = payloads[0]
    here = slice(s * SPAN, (s + 1) * SPAN)
    span = own[rows : rows + 1, s * SPAN : s * SPAN + 1].astype(f32)
    q = q_ref[here, at]

    def absorb(ref, top, diagonal, state):
        highest, total, summed = state
        keys = ref[pl.ds(top, rows), :HEAD_SIZE]
        values = ref[pl.ds(top, rows), HEAD_SIZE:]
        place = ref[pl.ds(top + rows, TAIL), :][:1].astype(f32)
        column = jnp.broadcast_to(place, (HEAD_SIZE, 2 * HEAD_SIZE)).T[:rows, :SPAN]
        allowed = column <= span
        if diagonal:
            key = lax.broadcasted_iota(jnp.int32, (rows, SPAN), 0)
            query = lax.broadcasted_iota(jnp.int32, (rows, SPAN), 1) + s * SPAN
            later = (key >= s * SPAN) & (key < (s + 1) * SPAN) & (key > query)
            allowed = allowed & jnp.logical_not(later)
        scores = jnp.where(allowed, nt(keys, q) * SCALE, negative_fill)
        newest = jnp.maximum(highest, jnp.max(scores, 0, keepdims=True))
        weights = jnp.where(allowed, jnp.exp(scores - newest), 0.0)
        factor = jnp.exp(highest - newest)
        total = total * factor + jnp.sum(weights, 0, keepdims=True)
        summed = summed * factor + jnp.dot(values.T, weights.astype(bf16), preferred_element_type=f32)
        return newest, total, summed

    state = (
        jnp.full((1, SPAN), negative_fill, f32),
        jnp.zeros((1, SPAN), f32),
        jnp.zeros((HEAD_SIZE, SPAN), f32),
    )
    for ref in payloads:
        if ref is own:
            state = absorb(ref, 0, True, state)
        else:
            block = rows + TAIL
            state = lax.fori_loop(
                0,
                ref.shape[0] // block,
                lambda i, state: absorb(ref, pl.multiple_of(i * block, TAIL), False, state),
                state,
            )
    ready_ref[here, at] = (state[2] / state[1]).T.astype(bf16)


def last_part(sums, queries, payloads, held, group_blocks):
    rows = queries.shape[0]
    heads = queries.shape[1] // HEAD_SIZE
    keys = sum(p.shape[0] for p in payloads[held:]) // (rows + TAIL) * rows
    return pl.pallas_call(
        functools.partial(last_kernel, held, group_blocks * rows),
        out_shape=jax.ShapeDtypeStruct(queries.shape, bf16),
        in_specs=[in_vmem] * (2 + len(payloads)),
        out_specs=in_hbm,
        scratch_shapes=[
            pltpu.VMEM((keys, HEAD_SIZE), bf16),
            pltpu.VMEM((SUMS, keys), bf16),
            pltpu.VMEM((TAIL, keys), bf16),
            pltpu.VMEM((SUMS, heads * SPAN) if keys > group_blocks * rows else (8, HEAD_SIZE), f32),
            pltpu.VMEM(queries.shape, bf16),
            pltpu.SemaphoreType.DMA((rows // SPAN,)),
        ],
        compiler_params=pltpu.CompilerParams(vmem_limit_bytes=VMEM_LIMIT),
        cost_estimate=pl.CostEstimate(
            flops=4 * rows * heads * keys * HEAD_SIZE,
            bytes_accessed=2 * rows * heads * HEAD_SIZE,
            transcendentals=rows * heads * keys,
        ),
    )(sums, queries, *payloads)


def swapped(block, bit):
    devices = range(lax.axis_size("ctx"))
    return lax.ppermute(block, "ctx", [(i ^ bit, i) for i in devices])


def body(queries, rotated_key_rows, value_state_rows, positions):
    heads_here = queries.shape[1] // HEAD_SIZE
    own = pack(rotated_key_rows, value_state_rows, positions, heads_here)
    size = lax.axis_size("ctx")
    if size == 4:
        core = swapped(own, 1)
        chip = swapped(own, 2)
        sums, q = first_part(queries, [own, core])
        chip, sums = lax.optimization_barrier((chip, sums))
        both = swapped(chip, 1)
        return last_part(sums, q, [own, core, chip, both], 2, 2)
    everyone = lax.all_gather(own, "ctx", axis=0)
    others = (lax.axis_index("ctx") + jnp.arange(1, size)) % size
    others = jnp.take(everyone, others, axis=0)
    rest = others[1:].reshape(-1, 2 * HEAD_SIZE)
    sums, q = first_part(queries, [own, others[0]])
    return last_part(sums, q, [own, others[0], rest], 2, 2)


def solution(mesh):
    placed = (P("ctx", "head"), P("ctx", None), P("ctx", None), P("ctx"))
    return jax.shard_map(
        body, mesh=mesh, in_specs=placed, out_specs=P("ctx", "head"), check_vma=False
    )
```

```python
import functools

import jax
import jax.numpy as jnp
from jax import lax
from jax.experimental import pallas as pl
from jax.experimental.pallas import tpu as pltpu
from jax.sharding import PartitionSpec as P

HEAD_SIZE = 128
QUERIES_PER_KV = 16
SPAN = 96
SCALE = HEAD_SIZE ** (-0.5)
SCALE_TWO = SCALE * 1.4426950408889634
TAIL = 16
SUMS = HEAD_SIZE + TAIL
negative_fill = -1e30
LEAST_TOTAL = 1e-25
LARGEST_TOTAL = 1e25
VMEM_LIMIT = 40 << 20

f32 = jnp.float32
bf16 = jnp.bfloat16
in_vmem = pl.BlockSpec(memory_space=pltpu.VMEM)
in_hbm = pl.BlockSpec(memory_space=pltpu.HBM)


def nt(a, b):
    return lax.dot_general(a, b, (((1,), (1,)), ((), ())), preferred_element_type=f32)


def tail_kernel(tail_ref):
    tail_ref[...] = jnp.zeros(tail_ref.shape, bf16)


def join_kernel(keys_ref, values_ref, positions_ref, tail_ref, block_ref):
    rows = keys_ref.shape[0]
    block_ref[:rows, :HEAD_SIZE] = keys_ref[...]
    block_ref[:rows, HEAD_SIZE:] = values_ref[...]
    places = jnp.floor((positions_ref[...].astype(f32) + 0.5) * (1.0 / SPAN))
    block_ref[rows:, :] = tail_ref[...]
    block_ref[rows:, :rows] = jnp.broadcast_to(places, (TAIL, rows)).astype(bf16)


def pack(keys, values, positions, heads):
    rows = keys.shape[0]
    group = lax.axis_index("head") * heads // QUERIES_PER_KV
    tail = pl.pallas_call(
        tail_kernel,
        out_shape=jax.ShapeDtypeStruct((TAIL, 2 * HEAD_SIZE), bf16),
        out_specs=in_vmem,
        compiler_params=pltpu.CompilerParams(vmem_limit_bytes=VMEM_LIMIT),
        cost_estimate=pl.CostEstimate(flops=2000000000, bytes_accessed=0, transcendentals=0),
    )()
    keys, values, tail = lax.optimization_barrier((keys, values, tail))
    ours = [lax.dynamic_slice_in_dim(a, group * HEAD_SIZE, HEAD_SIZE, 1) for a in (keys, values)]
    return pl.pallas_call(
        join_kernel,
        out_shape=jax.ShapeDtypeStruct((rows + TAIL, 2 * HEAD_SIZE), bf16),
        in_specs=[in_vmem] * 4,
        out_specs=in_vmem,
        compiler_params=pltpu.CompilerParams(vmem_limit_bytes=VMEM_LIMIT),
        cost_estimate=pl.CostEstimate(flops=2000000000, bytes_accessed=4 * rows * HEAD_SIZE, transcendentals=0),
    )(*ours, positions.reshape(1, rows), tail)


def blocks_of(payloads, rows):
    return [
        (ref, i * (rows + TAIL)) for ref in payloads for i in range(ref.shape[0] // (rows + TAIL))
    ]


def unpack(payloads, rows, keys_ref, values_ref, spans_ref):
    for at, (ref, top) in enumerate(blocks_of(payloads, rows)):
        here = slice(at * rows, (at + 1) * rows)
        keys_ref[here, :] = ref[top : top + rows, :HEAD_SIZE]
        values_ref[:HEAD_SIZE, here] = ref[top : top + rows, HEAD_SIZE:].T
        spans_ref[:, here] = ref[top + rows : top + rows + TAIL, :rows]
    values_ref[HEAD_SIZE:, :] = jnp.ones((TAIL, values_ref.shape[1]), bf16)


def stacked(q_ref, s, heads):
    here = slice(s * SPAN, (s + 1) * SPAN)
    return jnp.concatenate(
        [q_ref[here, h * HEAD_SIZE : (h + 1) * HEAD_SIZE] for h in range(heads)], 0
    )


def part(q, span, first, count, keys_ref, values_ref, spans_ref, own=None):
    some = pl.ds(first, count)
    allowed = (spans_ref[:1, some].astype(f32) <= span).astype(f32).astype(bf16)
    values = values_ref[:, some] * allowed
    weights = jnp.exp2(nt(keys_ref[some, :], q) * SCALE_TWO)
    if own is not None:
        key = lax.broadcasted_iota(jnp.int32, (SPAN, q.shape[0]), 0)
        query = lax.broadcasted_iota(jnp.int32, (SPAN, q.shape[0]), 1) % SPAN
        low, high = own * SPAN, (own + 1) * SPAN
        pieces = [weights[:low], jnp.where(key <= query, weights[low:high], 0.0), weights[high:]]
        weights = jnp.concatenate([p for p in pieces if p.shape[0]], 0)
    return jnp.dot(values, weights.astype(bf16), preferred_element_type=f32)


def first_kernel(q_ref, *refs):
    *payloads, sums_ref, keys_ref, values_ref, spans_ref = refs
    rows = q_ref.shape[0]
    heads = q_ref.shape[1] // HEAD_SIZE
    unpack(payloads, rows, keys_ref, values_ref, spans_ref)
    for s in range(rows // SPAN):
        span = spans_ref[:1, s * SPAN : s * SPAN + 1].astype(f32)
        sums_ref[s] = part(
            stacked(q_ref, s, heads), span, 0, keys_ref.shape[0], keys_ref, values_ref, spans_ref, s
        )


def first_part(queries, payloads):
    rows = queries.shape[0]
    heads = queries.shape[1] // HEAD_SIZE
    keys = sum(p.shape[0] for p in payloads) // (rows + TAIL) * rows
    return pl.pallas_call(
        first_kernel,
        out_shape=jax.ShapeDtypeStruct((rows // SPAN, SUMS, heads * SPAN), f32),
        in_specs=[in_vmem] * (1 + len(payloads)),
        out_specs=in_vmem,
        scratch_shapes=[
            pltpu.VMEM((keys, HEAD_SIZE), bf16),
            pltpu.VMEM((SUMS, keys), bf16),
            pltpu.VMEM((TAIL, keys), bf16),
        ],
        compiler_params=pltpu.CompilerParams(vmem_limit_bytes=VMEM_LIMIT),
        cost_estimate=pl.CostEstimate(
            flops=4 * rows * heads * keys * HEAD_SIZE,
            bytes_accessed=4 * rows * heads * HEAD_SIZE,
            transcendentals=rows * heads * keys,
        ),
    )(queries, *payloads)


def middle_kernel(sums_ref, q_ref, own_ref, *refs):
    *payloads, more_ref, keys_ref, values_ref, spans_ref = refs
    rows = q_ref.shape[0]
    heads = q_ref.shape[1] // HEAD_SIZE
    unpack(payloads, rows, keys_ref, values_ref, spans_ref)
    for s in range(rows // SPAN):
        span = own_ref[rows : rows + 1, s * SPAN : s * SPAN + 1].astype(f32)
        more_ref[s] = sums_ref[s] + part(
            stacked(q_ref, s, heads), span, 0, keys_ref.shape[0], keys_ref, values_ref, spans_ref
        )


def middle_part(sums, queries, own, payloads):
    rows = queries.shape[0]
    heads = queries.shape[1] // HEAD_SIZE
    keys = sum(p.shape[0] for p in payloads) // (rows + TAIL) * rows
    return pl.pallas_call(
        middle_kernel,
        out_shape=jax.ShapeDtypeStruct(sums.shape, f32),
        in_specs=[in_vmem] * (3 + len(payloads)),
        out_specs=in_vmem,
        scratch_shapes=[
            pltpu.VMEM((keys, HEAD_SIZE), bf16),
            pltpu.VMEM((SUMS, keys), bf16),
            pltpu.VMEM((TAIL, keys), bf16),
        ],
        input_output_aliases={0: 0},
        compiler_params=pltpu.CompilerParams(vmem_limit_bytes=VMEM_LIMIT),
        cost_estimate=pl.CostEstimate(
            flops=4 * rows * heads * keys * HEAD_SIZE,
            bytes_accessed=2 * rows * heads * HEAD_SIZE,
            transcendentals=rows * heads * keys,
        ),
    )(sums, queries, own, *payloads)


def last_kernel(held, group, sums_ref, q_ref, *refs):
    *payloads, out_ref, keys_ref, values_ref, spans_ref, acc_ref, ready_ref, sems = refs
    rows = q_ref.shape[0]
    heads = q_ref.shape[1] // HEAD_SIZE
    spans = rows // SPAN
    own = payloads[0]
    unpack(payloads[held:], rows, keys_ref, values_ref, spans_ref)
    groups = keys_ref.shape[0] // group

    def copy(s):
        here = pl.ds(s * SPAN, SPAN)
        return pltpu.make_async_copy(ready_ref.at[here, :], out_ref.at[here, :], sems.at[s])

    fine = None
    for s in range(spans):
        here = slice(s * SPAN, (s + 1) * SPAN)
        span = own[rows : rows + 1, s * SPAN : s * SPAN + 1].astype(f32)
        q = stacked(q_ref, s, heads)
        summed = sums_ref[s] + part(q, span, 0, group, keys_ref, values_ref, spans_ref)
        if groups > 1:
            acc_ref[...] = summed

            @pl.loop(1, groups)
            def _(g):
                first = pl.multiple_of(g * group, group)
                acc_ref[...] += part(q, span, first, group, keys_ref, values_ref, spans_ref)

            summed = acc_ref[...]
        total = summed[HEAD_SIZE : HEAD_SIZE + 1]
        inside = jnp.where((total >= LEAST_TOTAL) & (total <= LARGEST_TOTAL), 1.0, 0.0)
        fine = inside if fine is None else jnp.minimum(fine, inside)
        attended = (summed[:HEAD_SIZE] * (1.0 / total)).T.astype(bf16)
        for h in range(heads):
            ready_ref[here, h * HEAD_SIZE : (h + 1) * HEAD_SIZE] = attended[h * SPAN : (h + 1) * SPAN]
        copy(s).start()
    for s in range(spans):
        copy(s).wait()

    @pl.when(jnp.min(fine) < 0.5)
    def _():
        @pl.loop(0, heads)
        def _(h):
            at = pl.ds(pl.multiple_of(h * HEAD_SIZE, HEAD_SIZE), HEAD_SIZE)
            for s in range(spans):
                careful(payloads, q_ref, ready_ref, s, at)

        for s in range(spans):
            copy(s).start()
        for s in range(spans):
            copy(s).wait()


def careful(payloads, q_ref, ready_ref, s, at):
    rows = q_ref.shape[0]
    own = payloads[0]
    here = slice(s * SPAN, (s + 1) * SPAN)
    span = own[rows : rows + 1, s * SPAN : s * SPAN + 1].astype(f32)
    q = q_ref[here, at]

    def absorb(ref, top, diagonal, state):
        highest, total, summed = state
        keys = ref[pl.ds(top, rows), :HEAD_SIZE]
        values = ref[pl.ds(top, rows), HEAD_SIZE:]
        place = ref[pl.ds(top + rows, TAIL), :][:1].astype(f32)
        column = jnp.broadcast_to(place, (HEAD_SIZE, 2 * HEAD_SIZE)).T[:rows, :SPAN]
        allowed = column <= span
        if diagonal:
            key = lax.broadcasted_iota(jnp.int32, (rows, SPAN), 0)
            query = lax.broadcasted_iota(jnp.int32, (rows, SPAN), 1) + s * SPAN
            later = (key >= s * SPAN) & (key < (s + 1) * SPAN) & (key > query)
            allowed = allowed & jnp.logical_not(later)
        scores = jnp.where(allowed, nt(keys, q) * SCALE, negative_fill)
        newest = jnp.maximum(highest, jnp.max(scores, 0, keepdims=True))
        weights = jnp.where(allowed, jnp.exp(scores - newest), 0.0)
        factor = jnp.exp(highest - newest)
        total = total * factor + jnp.sum(weights, 0, keepdims=True)
        summed = summed * factor + jnp.dot(values.T, weights.astype(bf16), preferred_element_type=f32)
        return newest, total, summed

    state = (
        jnp.full((1, SPAN), negative_fill, f32),
        jnp.zeros((1, SPAN), f32),
        jnp.zeros((HEAD_SIZE, SPAN), f32),
    )
    for ref in payloads:
        if ref is own:
            state = absorb(ref, 0, True, state)
        else:
            block = rows + TAIL
            state = lax.fori_loop(
                0,
                ref.shape[0] // block,
                lambda i, state: absorb(ref, pl.multiple_of(i * block, TAIL), False, state),
                state,
            )
    ready_ref[here, at] = (state[2] / state[1]).T.astype(bf16)


def last_part(sums, queries, payloads, held, group_blocks):
    rows = queries.shape[0]
    heads = queries.shape[1] // HEAD_SIZE
    keys = sum(p.shape[0] for p in payloads[held:]) // (rows + TAIL) * rows
    return pl.pallas_call(
        functools.partial(last_kernel, held, group_blocks * rows),
        out_shape=jax.ShapeDtypeStruct(queries.shape, bf16),
        in_specs=[in_vmem] * (2 + len(payloads)),
        out_specs=in_hbm,
        scratch_shapes=[
            pltpu.VMEM((keys, HEAD_SIZE), bf16),
            pltpu.VMEM((SUMS, keys), bf16),
            pltpu.VMEM((TAIL, keys), bf16),
            pltpu.VMEM((SUMS, heads * SPAN) if keys > group_blocks * rows else (8, HEAD_SIZE), f32),
            pltpu.VMEM(queries.shape, bf16),
            pltpu.SemaphoreType.DMA((rows // SPAN,)),
        ],
        compiler_params=pltpu.CompilerParams(vmem_limit_bytes=VMEM_LIMIT),
        cost_estimate=pl.CostEstimate(
            flops=4 * rows * heads * keys * HEAD_SIZE,
            bytes_accessed=2 * rows * heads * HEAD_SIZE,
            transcendentals=rows * heads * keys,
        ),
    )(sums, queries, *payloads)


def swapped(block, bit):
    devices = range(lax.axis_size("ctx"))
    return lax.ppermute(block, "ctx", [(i ^ bit, i) for i in devices])


def body(queries, rotated_key_rows, value_state_rows, positions):
    own = pack(rotated_key_rows, value_state_rows, positions, queries.shape[1] // HEAD_SIZE)
    size = lax.axis_size("ctx")
    if size == 4:
        chip = swapped(own, 2)
        sums = first_part(queries, [own])
        again, sums = lax.optimization_barrier((own, sums))
        core = swapped(again, 1)
        both = swapped(chip, 1)
        sums = middle_part(sums, queries, own, [core, chip])
        return last_part(sums, queries, [own, core, chip, both], 3, 1)
    everyone = lax.all_gather(own, "ctx", axis=0)
    others = (lax.axis_index("ctx") + jnp.arange(1, size)) % size
    others = jnp.take(everyone, others, axis=0)
    rest = others[1:].reshape(-1, 2 * HEAD_SIZE)
    sums = first_part(queries, [own, others[0]])
    return last_part(sums, queries, [own, others[0], rest], 2, 2)


def solution(mesh):
    placed = (P("ctx", "head"), P("ctx", None), P("ctx", None), P("ctx"))
    return jax.shard_map(
        body, mesh=mesh, in_specs=placed, out_specs=P("ctx", "head"), check_vma=False
    )
```

```python
import functools

import jax
import jax.numpy as jnp
from jax import lax
from jax.experimental import pallas as pl
from jax.experimental.pallas import tpu as pltpu
from jax.sharding import PartitionSpec as P

HEAD_SIZE = 128
QUERIES_PER_KV = 16
SPAN = 96
SCALE = HEAD_SIZE ** (-0.5)
SCALE_TWO = SCALE * 1.4426950408889634
TAIL = 16
SUMS = HEAD_SIZE + TAIL
negative_fill = -1e30
LEAST_TOTAL = 1e-25
LARGEST_TOTAL = 1e25
VMEM_LIMIT = 40 << 20
PIECES = 2

f32 = jnp.float32
bf16 = jnp.bfloat16
in_vmem = pl.BlockSpec(memory_space=pltpu.VMEM)
in_hbm = pl.BlockSpec(memory_space=pltpu.HBM)


def nt(a, b):
    return lax.dot_general(a, b, (((1,), (1,)), ((), ())), preferred_element_type=f32)


def tail_kernel(tail_ref):
    tail_ref[...] = jnp.zeros(tail_ref.shape, bf16)


def join_kernel(keys_ref, values_ref, positions_ref, tail_ref, block_ref):
    rows = keys_ref.shape[0]
    block_ref[:rows, :HEAD_SIZE] = keys_ref[...]
    block_ref[:rows, HEAD_SIZE:] = values_ref[...]
    places = jnp.floor((positions_ref[...].astype(f32) + 0.5) * (1.0 / SPAN))
    block_ref[rows:, :] = tail_ref[...]
    block_ref[rows:, :rows] = jnp.broadcast_to(places, (TAIL, rows)).astype(bf16)


def pack(keys, values, positions, heads):
    rows = keys.shape[0]
    group = lax.axis_index("head") * heads // QUERIES_PER_KV
    tail = pl.pallas_call(
        tail_kernel,
        out_shape=jax.ShapeDtypeStruct((TAIL, 2 * HEAD_SIZE), bf16),
        out_specs=in_vmem,
        compiler_params=pltpu.CompilerParams(vmem_limit_bytes=VMEM_LIMIT),
        cost_estimate=pl.CostEstimate(flops=2000000000, bytes_accessed=0, transcendentals=0),
    )()
    keys, values, tail = lax.optimization_barrier((keys, values, tail))
    ours = [lax.dynamic_slice_in_dim(a, group * HEAD_SIZE, HEAD_SIZE, 1) for a in (keys, values)]
    return pl.pallas_call(
        join_kernel,
        out_shape=jax.ShapeDtypeStruct((rows + TAIL, 2 * HEAD_SIZE), bf16),
        in_specs=[in_vmem] * 4,
        out_specs=in_vmem,
        compiler_params=pltpu.CompilerParams(vmem_limit_bytes=VMEM_LIMIT),
        cost_estimate=pl.CostEstimate(flops=2000000000, bytes_accessed=4 * rows * HEAD_SIZE, transcendentals=0),
    )(*ours, positions.reshape(1, rows), tail)


def blocks_of(payloads, rows):
    return [
        (ref, i * (rows + TAIL)) for ref in payloads for i in range(ref.shape[0] // (rows + TAIL))
    ]


def unpack(payloads, rows, keys_ref, values_ref, spans_ref):
    for at, (ref, top) in enumerate(blocks_of(payloads, rows)):
        here = slice(at * rows, (at + 1) * rows)
        keys_ref[here, :] = ref[top : top + rows, :HEAD_SIZE]
        values_ref[:HEAD_SIZE, here] = ref[top : top + rows, HEAD_SIZE:].T
        spans_ref[:, here] = ref[top + rows : top + rows + TAIL, :rows]
    values_ref[HEAD_SIZE:, :] = jnp.ones((TAIL, values_ref.shape[1]), bf16)


def stacked(q_ref, s, heads):
    here = slice(s * SPAN, (s + 1) * SPAN)
    return jnp.concatenate(
        [q_ref[here, h * HEAD_SIZE : (h + 1) * HEAD_SIZE] for h in range(heads)], 0
    )


def part(q, span, first, count, keys_ref, values_ref, spans_ref, own=None):
    some = pl.ds(first, count)
    allowed = (spans_ref[:1, some].astype(f32) <= span).astype(f32).astype(bf16)
    values = values_ref[:, some] * allowed
    weights = jnp.exp2(nt(keys_ref[some, :], q) * SCALE_TWO)
    if own is not None:
        key = lax.broadcasted_iota(jnp.int32, (SPAN, q.shape[0]), 0)
        query = lax.broadcasted_iota(jnp.int32, (SPAN, q.shape[0]), 1) % SPAN
        low, high = own * SPAN, (own + 1) * SPAN
        pieces = [weights[:low], jnp.where(key <= query, weights[low:high], 0.0), weights[high:]]
        weights = jnp.concatenate([p for p in pieces if p.shape[0]], 0)
    return jnp.dot(values, weights.astype(bf16), preferred_element_type=f32)


def first_kernel(q_ref, *refs):
    *payloads, sums_ref, keys_ref, values_ref, spans_ref = refs
    rows = q_ref.shape[0]
    heads = q_ref.shape[1] // HEAD_SIZE
    unpack(payloads, rows, keys_ref, values_ref, spans_ref)
    for s in range(rows // SPAN):
        span = spans_ref[:1, s * SPAN : s * SPAN + 1].astype(f32)
        sums_ref[s] = part(
            stacked(q_ref, s, heads), span, 0, keys_ref.shape[0], keys_ref, values_ref, spans_ref, s
        )


def first_part(queries, payloads):
    rows = queries.shape[0]
    heads = queries.shape[1] // HEAD_SIZE
    keys = sum(p.shape[0] for p in payloads) // (rows + TAIL) * rows
    return pl.pallas_call(
        first_kernel,
        out_shape=jax.ShapeDtypeStruct((rows // SPAN, SUMS, heads * SPAN), f32),
        in_specs=[in_vmem] * (1 + len(payloads)),
        out_specs=in_vmem,
        scratch_shapes=[
            pltpu.VMEM((keys, HEAD_SIZE), bf16),
            pltpu.VMEM((SUMS, keys), bf16),
            pltpu.VMEM((TAIL, keys), bf16),
        ],
        compiler_params=pltpu.CompilerParams(vmem_limit_bytes=VMEM_LIMIT),
        cost_estimate=pl.CostEstimate(
            flops=4 * rows * heads * keys * HEAD_SIZE,
            bytes_accessed=4 * rows * heads * HEAD_SIZE,
            transcendentals=rows * heads * keys,
        ),
    )(queries, *payloads)


def middle_kernel(sums_ref, q_ref, own_ref, *refs):
    *payloads, more_ref, keys_ref, values_ref, spans_ref = refs
    rows = q_ref.shape[0]
    heads = q_ref.shape[1] // HEAD_SIZE
    unpack(payloads, rows, keys_ref, values_ref, spans_ref)
    for s in range(rows // SPAN):
        span = own_ref[rows : rows + 1, s * SPAN : s * SPAN + 1].astype(f32)
        more_ref[s] = sums_ref[s] + part(
            stacked(q_ref, s, heads), span, 0, keys_ref.shape[0], keys_ref, values_ref, spans_ref
        )


def middle_part(sums, queries, own, payloads):
    rows = queries.shape[0]
    heads = queries.shape[1] // HEAD_SIZE
    keys = sum(p.shape[0] for p in payloads) // (rows + TAIL) * rows
    return pl.pallas_call(
        middle_kernel,
        out_shape=jax.ShapeDtypeStruct(sums.shape, f32),
        in_specs=[in_vmem] * (3 + len(payloads)),
        out_specs=in_vmem,
        scratch_shapes=[
            pltpu.VMEM((keys, HEAD_SIZE), bf16),
            pltpu.VMEM((SUMS, keys), bf16),
            pltpu.VMEM((TAIL, keys), bf16),
        ],
        input_output_aliases={0: 0},
        compiler_params=pltpu.CompilerParams(vmem_limit_bytes=VMEM_LIMIT),
        cost_estimate=pl.CostEstimate(
            flops=4 * rows * heads * keys * HEAD_SIZE,
            bytes_accessed=2 * rows * heads * HEAD_SIZE,
            transcendentals=rows * heads * keys,
        ),
    )(sums, queries, own, *payloads)


def last_kernel(held, group, sums_ref, q_ref, *refs):
    *payloads, out_ref, keys_ref, values_ref, spans_ref, acc_ref, ready_ref, sems = refs
    rows = q_ref.shape[0]
    heads = q_ref.shape[1] // HEAD_SIZE
    spans = rows // SPAN
    own = payloads[0]
    unpack(payloads[held:], rows, keys_ref, values_ref, spans_ref)
    groups = keys_ref.shape[0] // group
    wide = q_ref.shape[1] // PIECES

    def copy(s, piece):
        at = (pl.ds(s * SPAN, SPAN), pl.ds(piece * wide, wide))
        return pltpu.make_async_copy(ready_ref.at[at], out_ref.at[at], sems.at[s, piece])

    fine = None
    for s in range(spans):
        here = slice(s * SPAN, (s + 1) * SPAN)
        span = own[rows : rows + 1, s * SPAN : s * SPAN + 1].astype(f32)
        q = stacked(q_ref, s, heads)
        summed = sums_ref[s] + part(q, span, 0, group, keys_ref, values_ref, spans_ref)
        if groups > 1:
            acc_ref[...] = summed

            @pl.loop(1, groups)
            def _(g):
                first = pl.multiple_of(g * group, group)
                acc_ref[...] += part(q, span, first, group, keys_ref, values_ref, spans_ref)

            summed = acc_ref[...]
        total = summed[HEAD_SIZE : HEAD_SIZE + 1]
        inside = jnp.where((total >= LEAST_TOTAL) & (total <= LARGEST_TOTAL), 1.0, 0.0)
        fine = inside if fine is None else jnp.minimum(fine, inside)
        inverse = 1.0 / total
        some = heads // PIECES
        for piece in range(PIECES):
            across = slice(piece * some * SPAN, (piece + 1) * some * SPAN)
            attended = (summed[:HEAD_SIZE, across] * inverse[:, across]).T.astype(bf16)
            for h in range(some):
                at = (piece * some + h) * HEAD_SIZE
                ready_ref[here, at : at + HEAD_SIZE] = attended[h * SPAN : (h + 1) * SPAN]
            copy(s, piece).start()
    unsafe = jnp.min(fine) < 0.5
    for s in range(spans):
        for piece in range(PIECES):
            copy(s, piece).wait()

    @pl.when(unsafe)
    def _():
        @pl.loop(0, heads)
        def _(h):
            at = pl.ds(pl.multiple_of(h * HEAD_SIZE, HEAD_SIZE), HEAD_SIZE)
            for s in range(spans):
                careful(payloads, q_ref, ready_ref, s, at)

        for s in range(spans):
            for piece in range(PIECES):
                copy(s, piece).start()
        for s in range(spans):
            for piece in range(PIECES):
                copy(s, piece).wait()


def careful(payloads, q_ref, ready_ref, s, at):
    rows = q_ref.shape[0]
    own = payloads[0]
    here = slice(s * SPAN, (s + 1) * SPAN)
    span = own[rows : rows + 1, s * SPAN : s * SPAN + 1].astype(f32)
    q = q_ref[here, at]

    def absorb(ref, top, diagonal, state):
        highest, total, summed = state
        keys = ref[pl.ds(top, rows), :HEAD_SIZE]
        values = ref[pl.ds(top, rows), HEAD_SIZE:]
        place = ref[pl.ds(top + rows, TAIL), :][:1].astype(f32)
        column = jnp.broadcast_to(place, (HEAD_SIZE, 2 * HEAD_SIZE)).T[:rows, :SPAN]
        allowed = column <= span
        if diagonal:
            key = lax.broadcasted_iota(jnp.int32, (rows, SPAN), 0)
            query = lax.broadcasted_iota(jnp.int32, (rows, SPAN), 1) + s * SPAN
            later = (key >= s * SPAN) & (key < (s + 1) * SPAN) & (key > query)
            allowed = allowed & jnp.logical_not(later)
        scores = jnp.where(allowed, nt(keys, q) * SCALE, negative_fill)
        newest = jnp.maximum(highest, jnp.max(scores, 0, keepdims=True))
        weights = jnp.where(allowed, jnp.exp(scores - newest), 0.0)
        factor = jnp.exp(highest - newest)
        total = total * factor + jnp.sum(weights, 0, keepdims=True)
        summed = summed * factor + jnp.dot(values.T, weights.astype(bf16), preferred_element_type=f32)
        return newest, total, summed

    state = (
        jnp.full((1, SPAN), negative_fill, f32),
        jnp.zeros((1, SPAN), f32),
        jnp.zeros((HEAD_SIZE, SPAN), f32),
    )
    for ref in payloads:
        if ref is own:
            state = absorb(ref, 0, True, state)
        else:
            block = rows + TAIL
            state = lax.fori_loop(
                0,
                ref.shape[0] // block,
                lambda i, state: absorb(ref, pl.multiple_of(i * block, TAIL), False, state),
                state,
            )
    ready_ref[here, at] = (state[2] / state[1]).T.astype(bf16)


def last_part(sums, queries, payloads, held, group_blocks):
    rows = queries.shape[0]
    heads = queries.shape[1] // HEAD_SIZE
    keys = sum(p.shape[0] for p in payloads[held:]) // (rows + TAIL) * rows
    return pl.pallas_call(
        functools.partial(last_kernel, held, group_blocks * rows),
        out_shape=jax.ShapeDtypeStruct(queries.shape, bf16),
        in_specs=[in_vmem] * (2 + len(payloads)),
        out_specs=in_hbm,
        scratch_shapes=[
            pltpu.VMEM((keys, HEAD_SIZE), bf16),
            pltpu.VMEM((SUMS, keys), bf16),
            pltpu.VMEM((TAIL, keys), bf16),
            pltpu.VMEM((SUMS, heads * SPAN) if keys > group_blocks * rows else (8, HEAD_SIZE), f32),
            pltpu.VMEM(queries.shape, bf16),
            pltpu.SemaphoreType.DMA((rows // SPAN, PIECES)),
        ],
        compiler_params=pltpu.CompilerParams(vmem_limit_bytes=VMEM_LIMIT),
        cost_estimate=pl.CostEstimate(
            flops=4 * rows * heads * keys * HEAD_SIZE,
            bytes_accessed=2 * rows * heads * HEAD_SIZE,
            transcendentals=rows * heads * keys,
        ),
    )(sums, queries, *payloads)


def swapped(block, bit):
    devices = range(lax.axis_size("ctx"))
    return lax.ppermute(block, "ctx", [(i ^ bit, i) for i in devices])


def body(queries, rotated_key_rows, value_state_rows, positions):
    own = pack(rotated_key_rows, value_state_rows, positions, queries.shape[1] // HEAD_SIZE)
    size = lax.axis_size("ctx")
    if size == 4:
        chip = swapped(own, 2)
        sums = first_part(queries, [own])
        again, sums = lax.optimization_barrier((own, sums))
        core = swapped(again, 1)
        both = swapped(chip, 1)
        sums = middle_part(sums, queries, own, [core, chip])
        return last_part(sums, queries, [own, core, chip, both], 3, 1)
    everyone = lax.all_gather(own, "ctx", axis=0)
    others = (lax.axis_index("ctx") + jnp.arange(1, size)) % size
    others = jnp.take(everyone, others, axis=0)
    rest = others[1:].reshape(-1, 2 * HEAD_SIZE)
    sums = first_part(queries, [own, others[0]])
    return last_part(sums, queries, [own, others[0], rest], 2, 2)


def solution(mesh):
    placed = (P("ctx", "head"), P("ctx", None), P("ctx", None), P("ctx"))
    return jax.shard_map(
        body, mesh=mesh, in_specs=placed, out_specs=P("ctx", "head"), check_vma=False
    )
```

```python
import functools

import jax
import jax.numpy as jnp
from jax import lax
from jax.experimental import pallas as pl
from jax.experimental.pallas import tpu as pltpu
from jax.sharding import PartitionSpec as P

HEAD_SIZE = 128
QUERIES_PER_KV = 16
SPAN = 96
SCALE = HEAD_SIZE ** (-0.5)
SCALE_TWO = SCALE * 1.4426950408889634
TAIL = 16
SUMS = HEAD_SIZE + TAIL
negative_fill = -1e30
LEAST_TOTAL = 1e-25
LARGEST_TOTAL = 1e25
VMEM_LIMIT = 40 << 20
PIECES = 2

f32 = jnp.float32
bf16 = jnp.bfloat16
in_vmem = pl.BlockSpec(memory_space=pltpu.VMEM)
in_hbm = pl.BlockSpec(memory_space=pltpu.HBM)


def nt(a, b):
    return lax.dot_general(a, b, (((1,), (1,)), ((), ())), preferred_element_type=f32)


def tail_kernel(tail_ref):
    tail_ref[...] = jnp.zeros(tail_ref.shape, bf16)


def join_kernel(keys_ref, values_ref, positions_ref, tail_ref, block_ref):
    rows = keys_ref.shape[0]
    block_ref[:rows, :HEAD_SIZE] = keys_ref[...]
    block_ref[:rows, HEAD_SIZE:] = values_ref[...]
    places = jnp.floor((positions_ref[...].astype(f32) + 0.5) * (1.0 / SPAN))
    block_ref[rows:, :] = tail_ref[...]
    block_ref[rows:, :rows] = jnp.broadcast_to(places, (TAIL, rows)).astype(bf16)


def pack(keys, values, positions, heads):
    rows = keys.shape[0]
    group = lax.axis_index("head") * heads // QUERIES_PER_KV
    tail = pl.pallas_call(
        tail_kernel,
        out_shape=jax.ShapeDtypeStruct((TAIL, 2 * HEAD_SIZE), bf16),
        out_specs=in_vmem,
        compiler_params=pltpu.CompilerParams(vmem_limit_bytes=VMEM_LIMIT),
        cost_estimate=pl.CostEstimate(flops=2000000000, bytes_accessed=0, transcendentals=0),
    )()
    keys, values, tail = lax.optimization_barrier((keys, values, tail))
    ours = [lax.dynamic_slice_in_dim(a, group * HEAD_SIZE, HEAD_SIZE, 1) for a in (keys, values)]
    return pl.pallas_call(
        join_kernel,
        out_shape=jax.ShapeDtypeStruct((rows + TAIL, 2 * HEAD_SIZE), bf16),
        in_specs=[in_vmem] * 4,
        out_specs=in_vmem,
        compiler_params=pltpu.CompilerParams(vmem_limit_bytes=VMEM_LIMIT),
        cost_estimate=pl.CostEstimate(flops=2000000000, bytes_accessed=4 * rows * HEAD_SIZE, transcendentals=0),
    )(*ours, positions.reshape(1, rows), tail)


def blocks_of(payloads, rows):
    return [
        (ref, i * (rows + TAIL)) for ref in payloads for i in range(ref.shape[0] // (rows + TAIL))
    ]


def unpack(payloads, rows, keys_ref, values_ref, spans_ref):
    for at, (ref, top) in enumerate(blocks_of(payloads, rows)):
        here = slice(at * rows, (at + 1) * rows)
        keys_ref[here, :] = ref[top : top + rows, :HEAD_SIZE]
        values_ref[:HEAD_SIZE, here] = ref[top : top + rows, HEAD_SIZE:].T
        spans_ref[:, here] = ref[top + rows : top + rows + TAIL, :rows]
    values_ref[HEAD_SIZE:, :] = jnp.ones((TAIL, values_ref.shape[1]), bf16)


def stacked(q_ref, s, heads):
    here = slice(s * SPAN, (s + 1) * SPAN)
    return jnp.concatenate(
        [q_ref[here, h * HEAD_SIZE : (h + 1) * HEAD_SIZE] for h in range(heads)], 0
    )


def part(q, span, first, count, keys_ref, values_ref, spans_ref, own=None):
    weights = weigh(q, first, count, keys_ref, own)
    return gather(weights, span, first, count, values_ref, spans_ref)


def gather(weights, span, first, count, values_ref, spans_ref):
    some = pl.ds(first, count)
    allowed = (spans_ref[:1, some].astype(f32) <= span).astype(f32).astype(bf16)
    values = values_ref[:, some] * allowed
    return jnp.dot(values, weights, preferred_element_type=f32)


def weigh(q, first, count, keys_ref, own=None):
    weights = jnp.exp2(nt(keys_ref[pl.ds(first, count), :], q) * SCALE_TWO)
    if own is not None:
        key = lax.broadcasted_iota(jnp.int32, (SPAN, q.shape[0]), 0)
        query = lax.broadcasted_iota(jnp.int32, (SPAN, q.shape[0]), 1) % SPAN
        low, high = own * SPAN, (own + 1) * SPAN
        pieces = [weights[:low], jnp.where(key <= query, weights[low:high], 0.0), weights[high:]]
        weights = jnp.concatenate([p for p in pieces if p.shape[0]], 0)
    return weights.astype(bf16)


def first_kernel(q_ref, *refs):
    *payloads, sums_ref, keys_ref, values_ref, spans_ref = refs
    rows = q_ref.shape[0]
    heads = q_ref.shape[1] // HEAD_SIZE
    unpack(payloads, rows, keys_ref, values_ref, spans_ref)
    keys = keys_ref.shape[0]
    weights = [weigh(stacked(q_ref, s, heads), 0, keys, keys_ref, s) for s in range(rows // SPAN)]
    for s, some in enumerate(weights):
        span = spans_ref[:1, s * SPAN : s * SPAN + 1].astype(f32)
        sums_ref[s] = gather(some, span, 0, keys, values_ref, spans_ref)


def first_part(queries, payloads):
    rows = queries.shape[0]
    heads = queries.shape[1] // HEAD_SIZE
    keys = sum(p.shape[0] for p in payloads) // (rows + TAIL) * rows
    return pl.pallas_call(
        first_kernel,
        out_shape=jax.ShapeDtypeStruct((rows // SPAN, SUMS, heads * SPAN), f32),
        in_specs=[in_vmem] * (1 + len(payloads)),
        out_specs=in_vmem,
        scratch_shapes=[
            pltpu.VMEM((keys, HEAD_SIZE), bf16),
            pltpu.VMEM((SUMS, keys), bf16),
            pltpu.VMEM((TAIL, keys), bf16),
        ],
        compiler_params=pltpu.CompilerParams(vmem_limit_bytes=VMEM_LIMIT),
        cost_estimate=pl.CostEstimate(
            flops=4 * rows * heads * keys * HEAD_SIZE,
            bytes_accessed=4 * rows * heads * HEAD_SIZE,
            transcendentals=rows * heads * keys,
        ),
    )(queries, *payloads)


def middle_kernel(sums_ref, q_ref, own_ref, *refs):
    *payloads, more_ref, keys_ref, values_ref, spans_ref = refs
    rows = q_ref.shape[0]
    heads = q_ref.shape[1] // HEAD_SIZE
    unpack(payloads, rows, keys_ref, values_ref, spans_ref)
    keys = keys_ref.shape[0]
    weights = [weigh(stacked(q_ref, s, heads), 0, keys, keys_ref) for s in range(rows // SPAN)]
    for s, some in enumerate(weights):
        span = own_ref[rows : rows + 1, s * SPAN : s * SPAN + 1].astype(f32)
        more_ref[s] = sums_ref[s] + gather(some, span, 0, keys, values_ref, spans_ref)


def middle_part(sums, queries, own, payloads):
    rows = queries.shape[0]
    heads = queries.shape[1] // HEAD_SIZE
    keys = sum(p.shape[0] for p in payloads) // (rows + TAIL) * rows
    return pl.pallas_call(
        middle_kernel,
        out_shape=jax.ShapeDtypeStruct(sums.shape, f32),
        in_specs=[in_vmem] * (3 + len(payloads)),
        out_specs=in_vmem,
        scratch_shapes=[
            pltpu.VMEM((keys, HEAD_SIZE), bf16),
            pltpu.VMEM((SUMS, keys), bf16),
            pltpu.VMEM((TAIL, keys), bf16),
        ],
        input_output_aliases={0: 0},
        compiler_params=pltpu.CompilerParams(vmem_limit_bytes=VMEM_LIMIT),
        cost_estimate=pl.CostEstimate(
            flops=4 * rows * heads * keys * HEAD_SIZE,
            bytes_accessed=2 * rows * heads * HEAD_SIZE,
            transcendentals=rows * heads * keys,
        ),
    )(sums, queries, own, *payloads)


def last_kernel(held, group, sums_ref, q_ref, *refs):
    *payloads, out_ref, keys_ref, values_ref, spans_ref, acc_ref, ready_ref, sems = refs
    rows = q_ref.shape[0]
    heads = q_ref.shape[1] // HEAD_SIZE
    spans = rows // SPAN
    own = payloads[0]
    unpack(payloads[held:], rows, keys_ref, values_ref, spans_ref)
    groups = keys_ref.shape[0] // group
    wide = q_ref.shape[1] // PIECES

    def copy(s, piece):
        at = (pl.ds(s * SPAN, SPAN), pl.ds(piece * wide, wide))
        return pltpu.make_async_copy(ready_ref.at[at], out_ref.at[at], sems.at[s, piece])

    weights = [weigh(stacked(q_ref, s, heads), 0, group, keys_ref) for s in range(spans if groups == 1 else 0)]
    sums = []
    for s in range(spans):
        span = own[rows : rows + 1, s * SPAN : s * SPAN + 1].astype(f32)
        if groups == 1:
            sums.append(sums_ref[s] + gather(weights[s], span, 0, group, values_ref, spans_ref))
            continue
        q = stacked(q_ref, s, heads)
        acc_ref[...] = sums_ref[s]

        @pl.loop(0, groups)
        def _(g):
            first = pl.multiple_of(g * group, group)
            acc_ref[...] += part(q, span, first, group, keys_ref, values_ref, spans_ref)

        sums.append(acc_ref[...])
    fine = None
    for s, summed in enumerate(sums):
        here = slice(s * SPAN, (s + 1) * SPAN)
        total = summed[HEAD_SIZE : HEAD_SIZE + 1]
        inside = jnp.where((total >= LEAST_TOTAL) & (total <= LARGEST_TOTAL), 1.0, 0.0)
        fine = inside if fine is None else jnp.minimum(fine, inside)
        inverse = 1.0 / total
        some = heads // PIECES
        for piece in range(PIECES):
            across = slice(piece * some * SPAN, (piece + 1) * some * SPAN)
            attended = (summed[:HEAD_SIZE, across] * inverse[:, across]).astype(bf16).T
            for h in range(some):
                at = (piece * some + h) * HEAD_SIZE
                ready_ref[here, at : at + HEAD_SIZE] = attended[h * SPAN : (h + 1) * SPAN]
            copy(s, piece).start()
    unsafe = jnp.min(fine) < 0.5
    for s in range(spans):
        for piece in range(PIECES):
            copy(s, piece).wait()

    @pl.when(unsafe)
    def _():
        @pl.loop(0, heads)
        def _(h):
            at = pl.ds(pl.multiple_of(h * HEAD_SIZE, HEAD_SIZE), HEAD_SIZE)
            for s in range(spans):
                careful(payloads, q_ref, ready_ref, s, at)

        for s in range(spans):
            for piece in range(PIECES):
                copy(s, piece).start()
        for s in range(spans):
            for piece in range(PIECES):
                copy(s, piece).wait()


def careful(payloads, q_ref, ready_ref, s, at):
    rows = q_ref.shape[0]
    own = payloads[0]
    here = slice(s * SPAN, (s + 1) * SPAN)
    span = own[rows : rows + 1, s * SPAN : s * SPAN + 1].astype(f32)
    q = q_ref[here, at]

    def absorb(ref, top, diagonal, state):
        highest, total, summed = state
        keys = ref[pl.ds(top, rows), :HEAD_SIZE]
        values = ref[pl.ds(top, rows), HEAD_SIZE:]
        place = ref[pl.ds(top + rows, TAIL), :][:1].astype(f32)
        column = jnp.broadcast_to(place, (HEAD_SIZE, 2 * HEAD_SIZE)).T[:rows, :SPAN]
        allowed = column <= span
        if diagonal:
            key = lax.broadcasted_iota(jnp.int32, (rows, SPAN), 0)
            query = lax.broadcasted_iota(jnp.int32, (rows, SPAN), 1) + s * SPAN
            later = (key >= s * SPAN) & (key < (s + 1) * SPAN) & (key > query)
            allowed = allowed & jnp.logical_not(later)
        scores = jnp.where(allowed, nt(keys, q) * SCALE, negative_fill)
        newest = jnp.maximum(highest, jnp.max(scores, 0, keepdims=True))
        weights = jnp.where(allowed, jnp.exp(scores - newest), 0.0)
        factor = jnp.exp(highest - newest)
        total = total * factor + jnp.sum(weights, 0, keepdims=True)
        summed = summed * factor + jnp.dot(values.T, weights.astype(bf16), preferred_element_type=f32)
        return newest, total, summed

    state = (
        jnp.full((1, SPAN), negative_fill, f32),
        jnp.zeros((1, SPAN), f32),
        jnp.zeros((HEAD_SIZE, SPAN), f32),
    )
    for ref in payloads:
        if ref is own:
            state = absorb(ref, 0, True, state)
        else:
            block = rows + TAIL
            state = lax.fori_loop(
                0,
                ref.shape[0] // block,
                lambda i, state: absorb(ref, pl.multiple_of(i * block, TAIL), False, state),
                state,
            )
    ready_ref[here, at] = (state[2] / state[1]).T.astype(bf16)


def last_part(sums, queries, payloads, held, group_blocks):
    rows = queries.shape[0]
    heads = queries.shape[1] // HEAD_SIZE
    keys = sum(p.shape[0] for p in payloads[held:]) // (rows + TAIL) * rows
    return pl.pallas_call(
        functools.partial(last_kernel, held, group_blocks * rows),
        out_shape=jax.ShapeDtypeStruct(queries.shape, bf16),
        in_specs=[in_vmem] * (2 + len(payloads)),
        out_specs=in_hbm,
        scratch_shapes=[
            pltpu.VMEM((keys, HEAD_SIZE), bf16),
            pltpu.VMEM((SUMS, keys), bf16),
            pltpu.VMEM((TAIL, keys), bf16),
            pltpu.VMEM((SUMS, heads * SPAN) if keys > group_blocks * rows else (8, HEAD_SIZE), f32),
            pltpu.VMEM(queries.shape, bf16),
            pltpu.SemaphoreType.DMA((rows // SPAN, PIECES)),
        ],
        compiler_params=pltpu.CompilerParams(vmem_limit_bytes=VMEM_LIMIT),
        cost_estimate=pl.CostEstimate(
            flops=4 * rows * heads * keys * HEAD_SIZE,
            bytes_accessed=2 * rows * heads * HEAD_SIZE,
            transcendentals=rows * heads * keys,
        ),
    )(sums, queries, *payloads)


def swapped(block, bit):
    devices = range(lax.axis_size("ctx"))
    return lax.ppermute(block, "ctx", [(i ^ bit, i) for i in devices])


def body(queries, rotated_key_rows, value_state_rows, positions):
    own = pack(rotated_key_rows, value_state_rows, positions, queries.shape[1] // HEAD_SIZE)
    size = lax.axis_size("ctx")
    if size == 4:
        chip = swapped(own, 2)
        sums = first_part(queries, [own])
        again, sums = lax.optimization_barrier((own, sums))
        core = swapped(again, 1)
        both = swapped(chip, 1)
        sums = middle_part(sums, queries, own, [core, chip])
        return last_part(sums, queries, [own, core, chip, both], 3, 1)
    everyone = lax.all_gather(own, "ctx", axis=0)
    others = (lax.axis_index("ctx") + jnp.arange(1, size)) % size
    others = jnp.take(everyone, others, axis=0)
    rest = others[1:].reshape(-1, 2 * HEAD_SIZE)
    sums = first_part(queries, [own, others[0]])
    return last_part(sums, queries, [own, others[0], rest], 2, 2)


def solution(mesh):
    placed = (P("ctx", "head"), P("ctx", None), P("ctx", None), P("ctx"))
    return jax.shard_map(
        body, mesh=mesh, in_specs=placed, out_specs=P("ctx", "head"), check_vma=False
    )
```

```python
import functools

import jax
import jax.numpy as jnp
from jax import lax
from jax.experimental import pallas as pl
from jax.experimental.pallas import tpu as pltpu
from jax.sharding import PartitionSpec as P

HEAD_SIZE = 128
QUERIES_PER_KV = 16
SPAN = 96
SCALE = HEAD_SIZE ** (-0.5)
SCALE_TWO = SCALE * 1.4426950408889634
TAIL = 16
SUMS = HEAD_SIZE + TAIL
negative_fill = -1e30
LEAST_TOTAL = 1e-25
LARGEST_TOTAL = 1e25
VMEM_LIMIT = 40 << 20
PIECES = 2

f32 = jnp.float32
bf16 = jnp.bfloat16
in_vmem = pl.BlockSpec(memory_space=pltpu.VMEM)
in_hbm = pl.BlockSpec(memory_space=pltpu.HBM)


def nt(a, b):
    return lax.dot_general(a, b, (((1,), (1,)), ((), ())), preferred_element_type=f32)


def tail_kernel(tail_ref):
    tail_ref[...] = jnp.zeros(tail_ref.shape, bf16)


def join_kernel(keys_ref, values_ref, positions_ref, tail_ref, block_ref):
    rows = keys_ref.shape[0]
    block_ref[:rows, :HEAD_SIZE] = keys_ref[...]
    block_ref[:rows, HEAD_SIZE:] = values_ref[...]
    places = jnp.floor((positions_ref[...].astype(f32) + 0.5) * (1.0 / SPAN))
    block_ref[rows:, :] = tail_ref[...]
    block_ref[rows:, :rows] = jnp.broadcast_to(places, (TAIL, rows)).astype(bf16)


def pack(keys, values, positions, heads):
    rows = keys.shape[0]
    group = lax.axis_index("head") * heads // QUERIES_PER_KV
    tail = pl.pallas_call(
        tail_kernel,
        out_shape=jax.ShapeDtypeStruct((TAIL, 2 * HEAD_SIZE), bf16),
        out_specs=in_vmem,
        compiler_params=pltpu.CompilerParams(vmem_limit_bytes=VMEM_LIMIT),
        cost_estimate=pl.CostEstimate(flops=2000000000, bytes_accessed=0, transcendentals=0),
    )()
    keys, values, tail = lax.optimization_barrier((keys, values, tail))
    ours = [lax.dynamic_slice_in_dim(a, group * HEAD_SIZE, HEAD_SIZE, 1) for a in (keys, values)]
    return pl.pallas_call(
        join_kernel,
        out_shape=jax.ShapeDtypeStruct((rows + TAIL, 2 * HEAD_SIZE), bf16),
        in_specs=[in_vmem] * 4,
        out_specs=in_vmem,
        compiler_params=pltpu.CompilerParams(vmem_limit_bytes=VMEM_LIMIT),
        cost_estimate=pl.CostEstimate(flops=2000000000, bytes_accessed=4 * rows * HEAD_SIZE, transcendentals=0),
    )(*ours, positions.reshape(1, rows), tail)


def blocks_of(payloads, rows):
    return [
        (ref, i * (rows + TAIL)) for ref in payloads for i in range(ref.shape[0] // (rows + TAIL))
    ]


def unpack(payloads, rows, keys_ref, values_ref, spans_ref):
    for at, (ref, top) in enumerate(blocks_of(payloads, rows)):
        here = slice(at * rows, (at + 1) * rows)
        keys_ref[here, :] = ref[top : top + rows, :HEAD_SIZE]
        values_ref[:HEAD_SIZE, here] = ref[top : top + rows, HEAD_SIZE:].T
        spans_ref[:, here] = ref[top + rows : top + rows + TAIL, :rows]
    values_ref[HEAD_SIZE:, :] = jnp.ones((TAIL, values_ref.shape[1]), bf16)


def stacked(q_ref, s, heads):
    here = slice(s * SPAN, (s + 1) * SPAN)
    return jnp.concatenate(
        [q_ref[here, h * HEAD_SIZE : (h + 1) * HEAD_SIZE] for h in range(heads)], 0
    )


def part(q, span, first, count, keys_ref, values_ref, spans_ref, own=None):
    weights = weigh(q, first, count, keys_ref, own)
    return gather(weights, span, first, count, values_ref, spans_ref)


def gather(weights, span, first, count, values_ref, spans_ref):
    some = pl.ds(first, count)
    allowed = (spans_ref[:1, some].astype(f32) <= span).astype(f32).astype(bf16)
    values = values_ref[:, some] * allowed
    return jnp.dot(values, weights, preferred_element_type=f32)


def weigh(q, first, count, keys_ref, own=None):
    weights = jnp.exp2(nt(keys_ref[pl.ds(first, count), :], q) * SCALE_TWO)
    if own is not None:
        key = lax.broadcasted_iota(jnp.int32, (SPAN, q.shape[0]), 0)
        query = lax.broadcasted_iota(jnp.int32, (SPAN, q.shape[0]), 1) % SPAN
        low, high = own * SPAN, (own + 1) * SPAN
        pieces = [weights[:low], jnp.where(key <= query, weights[low:high], 0.0), weights[high:]]
        weights = jnp.concatenate([p for p in pieces if p.shape[0]], 0)
    return weights.astype(bf16)


def first_kernel(q_ref, *refs):
    *payloads, sums_ref, keys_ref, values_ref, spans_ref = refs
    rows = q_ref.shape[0]
    heads = q_ref.shape[1] // HEAD_SIZE
    unpack(payloads, rows, keys_ref, values_ref, spans_ref)
    keys = keys_ref.shape[0]
    weights = [weigh(stacked(q_ref, s, heads), 0, keys, keys_ref, s) for s in range(rows // SPAN)]
    for s, some in enumerate(weights):
        span = spans_ref[:1, s * SPAN : s * SPAN + 1].astype(f32)
        sums_ref[s] = gather(some, span, 0, keys, values_ref, spans_ref)


def first_part(queries, payloads):
    rows = queries.shape[0]
    heads = queries.shape[1] // HEAD_SIZE
    keys = sum(p.shape[0] for p in payloads) // (rows + TAIL) * rows
    return pl.pallas_call(
        first_kernel,
        out_shape=jax.ShapeDtypeStruct((rows // SPAN, SUMS, heads * SPAN), f32),
        in_specs=[in_vmem] * (1 + len(payloads)),
        out_specs=in_vmem,
        scratch_shapes=[
            pltpu.VMEM((keys, HEAD_SIZE), bf16),
            pltpu.VMEM((SUMS, keys), bf16),
            pltpu.VMEM((TAIL, keys), bf16),
        ],
        compiler_params=pltpu.CompilerParams(vmem_limit_bytes=VMEM_LIMIT),
        cost_estimate=pl.CostEstimate(
            flops=4 * rows * heads * keys * HEAD_SIZE,
            bytes_accessed=4 * rows * heads * HEAD_SIZE,
            transcendentals=rows * heads * keys,
        ),
    )(queries, *payloads)


def middle_kernel(sums_ref, q_ref, own_ref, *refs):
    *payloads, more_ref, keys_ref, values_ref, spans_ref = refs
    rows = q_ref.shape[0]
    heads = q_ref.shape[1] // HEAD_SIZE
    unpack(payloads, rows, keys_ref, values_ref, spans_ref)
    keys = keys_ref.shape[0]
    weights = [weigh(stacked(q_ref, s, heads), 0, keys, keys_ref) for s in range(rows // SPAN)]
    for s, some in enumerate(weights):
        span = own_ref[rows : rows + 1, s * SPAN : s * SPAN + 1].astype(f32)
        more_ref[s] = sums_ref[s] + gather(some, span, 0, keys, values_ref, spans_ref)


def middle_part(sums, queries, own, payloads):
    rows = queries.shape[0]
    heads = queries.shape[1] // HEAD_SIZE
    keys = sum(p.shape[0] for p in payloads) // (rows + TAIL) * rows
    return pl.pallas_call(
        middle_kernel,
        out_shape=jax.ShapeDtypeStruct(sums.shape, f32),
        in_specs=[in_vmem] * (3 + len(payloads)),
        out_specs=in_vmem,
        scratch_shapes=[
            pltpu.VMEM((keys, HEAD_SIZE), bf16),
            pltpu.VMEM((SUMS, keys), bf16),
            pltpu.VMEM((TAIL, keys), bf16),
        ],
        compiler_params=pltpu.CompilerParams(vmem_limit_bytes=VMEM_LIMIT),
        cost_estimate=pl.CostEstimate(
            flops=4 * rows * heads * keys * HEAD_SIZE,
            bytes_accessed=2 * rows * heads * HEAD_SIZE,
            transcendentals=rows * heads * keys,
        ),
    )(sums, queries, own, *payloads)


def last_kernel(held, group, sums_ref, q_ref, *refs):
    *payloads, out_ref, keys_ref, values_ref, spans_ref, acc_ref, ready_ref, sems = refs
    rows = q_ref.shape[0]
    heads = q_ref.shape[1] // HEAD_SIZE
    spans = rows // SPAN
    own = payloads[0]
    unpack(payloads[held:], rows, keys_ref, values_ref, spans_ref)
    groups = keys_ref.shape[0] // group
    wide = q_ref.shape[1] // PIECES

    def copy(s, piece):
        at = (pl.ds(s * SPAN, SPAN), pl.ds(piece * wide, wide))
        return pltpu.make_async_copy(ready_ref.at[at], out_ref.at[at], sems.at[s, piece])

    weights = [weigh(stacked(q_ref, s, heads), 0, group, keys_ref) for s in range(spans if groups == 1 else 0)]
    sums = []
    for s in range(spans):
        span = own[rows : rows + 1, s * SPAN : s * SPAN + 1].astype(f32)
        if groups == 1:
            sums.append(sums_ref[s] + gather(weights[s], span, 0, group, values_ref, spans_ref))
            continue
        q = stacked(q_ref, s, heads)
        acc_ref[...] = sums_ref[s]

        @pl.loop(0, groups)
        def _(g):
            first = pl.multiple_of(g * group, group)
            acc_ref[...] += part(q, span, first, group, keys_ref, values_ref, spans_ref)

        sums.append(acc_ref[...])
    fine = None
    for s, summed in enumerate(sums):
        here = slice(s * SPAN, (s + 1) * SPAN)
        total = summed[HEAD_SIZE : HEAD_SIZE + 1]
        inside = jnp.where((total >= LEAST_TOTAL) & (total <= LARGEST_TOTAL), 1.0, 0.0)
        fine = inside if fine is None else jnp.minimum(fine, inside)
        inverse = 1.0 / total
        some = heads // PIECES
        for piece in range(PIECES):
            across = slice(piece * some * SPAN, (piece + 1) * some * SPAN)
            attended = (summed[:HEAD_SIZE, across] * inverse[:, across]).astype(bf16).T
            for h in range(some):
                at = (piece * some + h) * HEAD_SIZE
                ready_ref[here, at : at + HEAD_SIZE] = attended[h * SPAN : (h + 1) * SPAN]
            copy(s, piece).start()
    unsafe = jnp.min(fine) < 0.5
    for s in range(spans):
        for piece in range(PIECES):
            copy(s, piece).wait()

    @pl.when(unsafe)
    def _():
        @pl.loop(0, heads)
        def _(h):
            at = pl.ds(pl.multiple_of(h * HEAD_SIZE, HEAD_SIZE), HEAD_SIZE)
            for s in range(spans):
                careful(payloads, q_ref, ready_ref, s, at)

        for s in range(spans):
            for piece in range(PIECES):
                copy(s, piece).start()
        for s in range(spans):
            for piece in range(PIECES):
                copy(s, piece).wait()


def careful(payloads, q_ref, ready_ref, s, at):
    rows = q_ref.shape[0]
    own = payloads[0]
    here = slice(s * SPAN, (s + 1) * SPAN)
    span = own[rows : rows + 1, s * SPAN : s * SPAN + 1].astype(f32)
    q = q_ref[here, at]

    def absorb(ref, top, diagonal, state):
        highest, total, summed = state
        keys = ref[pl.ds(top, rows), :HEAD_SIZE]
        values = ref[pl.ds(top, rows), HEAD_SIZE:]
        place = ref[pl.ds(top + rows, TAIL), :][:1].astype(f32)
        column = jnp.broadcast_to(place, (HEAD_SIZE, 2 * HEAD_SIZE)).T[:rows, :SPAN]
        allowed = column <= span
        if diagonal:
            key = lax.broadcasted_iota(jnp.int32, (rows, SPAN), 0)
            query = lax.broadcasted_iota(jnp.int32, (rows, SPAN), 1) + s * SPAN
            later = (key >= s * SPAN) & (key < (s + 1) * SPAN) & (key > query)
            allowed = allowed & jnp.logical_not(later)
        scores = jnp.where(allowed, nt(keys, q) * SCALE, negative_fill)
        newest = jnp.maximum(highest, jnp.max(scores, 0, keepdims=True))
        weights = jnp.where(allowed, jnp.exp(scores - newest), 0.0)
        factor = jnp.exp(highest - newest)
        total = total * factor + jnp.sum(weights, 0, keepdims=True)
        summed = summed * factor + jnp.dot(values.T, weights.astype(bf16), preferred_element_type=f32)
        return newest, total, summed

    state = (
        jnp.full((1, SPAN), negative_fill, f32),
        jnp.zeros((1, SPAN), f32),
        jnp.zeros((HEAD_SIZE, SPAN), f32),
    )
    for ref in payloads:
        if ref is own:
            state = absorb(ref, 0, True, state)
        else:
            block = rows + TAIL
            state = lax.fori_loop(
                0,
                ref.shape[0] // block,
                lambda i, state: absorb(ref, pl.multiple_of(i * block, TAIL), False, state),
                state,
            )
    ready_ref[here, at] = (state[2] / state[1]).T.astype(bf16)


def last_part(sums, queries, payloads, held, group_blocks):
    rows = queries.shape[0]
    heads = queries.shape[1] // HEAD_SIZE
    keys = sum(p.shape[0] for p in payloads[held:]) // (rows + TAIL) * rows
    return pl.pallas_call(
        functools.partial(last_kernel, held, group_blocks * rows),
        out_shape=jax.ShapeDtypeStruct(queries.shape, bf16),
        in_specs=[in_vmem] * (2 + len(payloads)),
        out_specs=in_hbm,
        scratch_shapes=[
            pltpu.VMEM((keys, HEAD_SIZE), bf16),
            pltpu.VMEM((SUMS, keys), bf16),
            pltpu.VMEM((TAIL, keys), bf16),
            pltpu.VMEM((SUMS, heads * SPAN) if keys > group_blocks * rows else (8, HEAD_SIZE), f32),
            pltpu.VMEM(queries.shape, bf16),
            pltpu.SemaphoreType.DMA((rows // SPAN, PIECES)),
        ],
        compiler_params=pltpu.CompilerParams(vmem_limit_bytes=VMEM_LIMIT),
        cost_estimate=pl.CostEstimate(
            flops=4 * rows * heads * keys * HEAD_SIZE,
            bytes_accessed=2 * rows * heads * HEAD_SIZE,
            transcendentals=rows * heads * keys,
        ),
    )(sums, queries, *payloads)


def swapped(block, bit):
    devices = range(lax.axis_size("ctx"))
    return lax.ppermute(block, "ctx", [(i ^ bit, i) for i in devices])


def body(queries, rotated_key_rows, value_state_rows, positions):
    own = pack(rotated_key_rows, value_state_rows, positions, queries.shape[1] // HEAD_SIZE)
    size = lax.axis_size("ctx")
    if size == 4:
        chip = swapped(own, 2)
        sums = first_part(queries, [own])
        again, sums = lax.optimization_barrier((own, sums))
        core = swapped(again, 1)
        both = swapped(chip, 1)
        sums = middle_part(sums, queries, own, [core, chip])
        return last_part(sums, queries, [own, core, chip, both], 3, 1)
    everyone = lax.all_gather(own, "ctx", axis=0)
    others = (lax.axis_index("ctx") + jnp.arange(1, size)) % size
    others = jnp.take(everyone, others, axis=0)
    rest = others[1:].reshape(-1, 2 * HEAD_SIZE)
    sums = first_part(queries, [own, others[0]])
    return last_part(sums, queries, [own, others[0], rest], 2, 2)


def solution(mesh):
    placed = (P("ctx", "head"), P("ctx", None), P("ctx", None), P("ctx"))
    return jax.shard_map(
        body, mesh=mesh, in_specs=placed, out_specs=P("ctx", "head"), check_vma=False
    )
```
